256 devices in a mesh: gz: 8 (over y, core), xy: 32 (over z, x).
Axes of the slice: x: 4, y: 4, z: 8, core: 2. Of those that a mesh axis runs over, the one named last changes fastest.
Arguments:
- right_side: float32 [12, 16, 64, 512], P(None, 'gz', 'xy'), may hold values from -24 to 24
- jac_diag: bfloat16 [12, 12, 16, 64, 512], P(None, None, 'gz', 'xy'), may hold values from -1.25 to 7.05
- jac_off: bfloat16 [6, 12, 12, 16, 64, 512], P(None, None, None, 'gz', 'xy'), may hold values from -0.59765625 to 0.59765625
- block_inv: bfloat16 [12, 12, 16, 64, 512], P(None, None, 'gz', 'xy'), may hold values from -0.125 to 0.405
- press_weight: bfloat16 [12, 16, 64, 512], P(None, 'gz', 'xy'), may hold values from 0.099609375 to 1
- press_diag: bfloat16 [16, 64, 512], P('gz', 'xy'), may hold values from 6.5 to 9
- press_off: bfloat16 [6, 16, 64, 512], P(None, 'gz', 'xy'), may hold values from -1 to -0.19921875
- well_index: float32 [16, 64, 512], P('gz', 'xy'), may hold values from 0.5 to 5
- well_columns: int32 [64], replicated, may hold values from 0 to 32767
- agg_map: int32 [16, 64, 512], P('gz', 'xy'), may hold values from 0 to 7
- level1_op: bfloat16 [8, 8, 16, 64, 4], P(None, None, 'gz', 'xy'), may hold values from -1.65 to 5.05
- coarsest_inv: bfloat16 [16, 64, 16, 64], P('gz', 'xy'), may hold values from -0.13479223 to 0.31156893
Outputs:
- solution: float32 [12, 16, 64, 512], P(None, 'gz', 'xy')
- residual: float32 [12, 16, 64, 512], P(None, 'gz', 'xy')
- hessenberg: float32 [3, 2], replicated
The draws below stay inside these ranges and needn't reach their ends.
Inputs may be any that keep to these rules, and one draw needn't show every extreme that they name: `well_columns`: flat areal index x * 512 + y of each vertical well, which is perforated in every layer; a column may hold several wells. `agg_map`: an aggregate may be empty.
All inputs are finite; a program needn't handle non-finite values.
Results may differ from the reference program's by a relative error of at most 0.0018.
Values may be sent and summed in bfloat16 or wider, within the bound.
No kernel may reach another device: no remote copies, remote signals or barrier semaphores. Data moves between devices by JAX's collectives and lax.ppermute only.
A program may use at most 64 MiB of HBM per device.

```python
import math
import jax
import jax.numpy as jnp
from jax import lax

NC = 12
NY = 512
BLK = 128
AGG = 8
NW = 64
ITERS = 2
NZ = 16
NX = 64
NB = 4


def diagonal_blocks(key, count, trailing, low, high, noise_scale):
    noise_key, middle_key = jax.random.split(key)
    shape = (count, count) + trailing
    noise = noise_scale * jnp.clip(jax.random.normal(noise_key, shape, jnp.float32), -4.0, 4.0)
    middle = jax.random.uniform(middle_key, (count,) + trailing, jnp.float32, low, high)
    identity = jnp.eye(count, dtype=jnp.float32).reshape((count, count) + (1,) * len(trailing))
    return noise * (1.0 - identity) + identity * middle[None]


def draw_jac_diag(key, part):
    blocks = diagonal_blocks(key, NC, (NZ, NX, NY), 3.0, 6.0, 0.3)
    return blocks.astype(jnp.bfloat16)


def draw_block_inv(key, part):
    blocks = diagonal_blocks(key, NC, (NZ, NX, NY), 0.17, 0.33, 0.03)
    return blocks.astype(jnp.bfloat16)


def draw_level1_op(key, part):
    blocks = diagonal_blocks(key, AGG, (NZ, NX, NB), 2.0, 4.0, 0.4)
    return blocks.astype(jnp.bfloat16)


def draw_coarsest_inv(key, part):
    order = NZ * NX
    scale = NY ** (-0.5)
    spread = scale * order ** (-0.5)
    blocks = diagonal_blocks(key, order, (), 3.0 * scale, 6.0 * scale, 3.6 * spread)
    return blocks.reshape(NZ, NX, NZ, NX).astype(jnp.bfloat16)


def touch_ends(values, rng, least, largest):
    place = [jax.random.randint(jax.random.fold_in(rng, axis), (), 0, length) for axis, length in enumerate(values.shape)]
    longest = values.shape.index(max(values.shape))
    beside = place[:longest] + [(place[longest] + 1) % values.shape[longest]] + place[longest + 1:]
    return values.at[tuple(place)].set(least).at[tuple(beside)].set(largest)


def block_scale(own_key, extent, pieces, smallest, largest):
    loudness, own = 1.0, jax.random.fold_in(own_key, 6)
    for axis_at, parts in pieces:
        draws = jnp.exp(jax.random.uniform(jax.random.fold_in(own, axis_at), (parts,), jnp.float32, smallest / len(pieces), largest / len(pieces)))
        loudness = loudness * jnp.repeat(draws, extent[axis_at] // parts).reshape([-1 if axis == axis_at else 1 for axis in range(len(extent))])
    return loudness


def scatter_about(rng, shape, deviation, most, shards=(), kind=jnp.bfloat16):
    values = jax.random.normal(rng, shape, jnp.float32) * deviation
    if len(shards) > 0:
        values = block_scale(rng, shape, shards, -0.22, 0.18) * values
    return jnp.clip(values, min=-most, max=most).astype(kind)


def setup_inputs(seed: int = 0) -> dict:
    arg_keys = jax.random.split(jax.random.key(seed), 13)
    right_side = scatter_about(arg_keys[0], (NC, NZ, NX, NY), 4.0, 24.0, ((1, 8), (2, 32)), jnp.float32)
    jac_diag = draw_jac_diag(jax.random.fold_in(arg_keys[12], 71), 0)
    jac_off = scatter_about(arg_keys[2], (6, NC, NC, NZ, NX, NY), 0.1, 0.59765625, ((3, 8), (4, 32)))
    block_inv = draw_block_inv(jax.random.fold_in(arg_keys[12], 71), 0)
    press_weight = jnp.clip(0.099609375 + 0.9003906 * jax.random.uniform(arg_keys[4], (NC, NZ, NX, NY), jnp.float32) ** block_scale(arg_keys[4], (NC, NZ, NX, NY), ((1, 8), (2, 32)), -0.2, 0.2), 0.099609375, 1.0).astype(jnp.bfloat16)
    press_diag = jnp.clip(6.5 + 2.5 * jax.random.uniform(arg_keys[5], (NZ, NX, NY), jnp.float32) ** block_scale(arg_keys[5], (NZ, NX, NY), ((0, 8), (1, 32)), -0.2, 0.2), 6.5, 9.0).astype(jnp.bfloat16)
    press_off = jnp.clip(-1.0 + 0.80078125 * jax.random.uniform(arg_keys[6], (6, NZ, NX, NY), jnp.float32) ** block_scale(arg_keys[6], (6, NZ, NX, NY), ((1, 8), (2, 32)), -0.2, 0.2), -1.0, -0.19921875).astype(jnp.bfloat16)
    well_index = jnp.clip(jnp.exp(math.log(5.0) - 2.3025851 * jax.random.uniform(arg_keys[7], (NZ, NX, NY), jnp.float32) ** block_scale(arg_keys[7], (NZ, NX, NY), ((0, 8), (1, 32)), -0.2, 0.2)), 0.5, 5.0)
    well_columns = touch_ends(jax.random.randint(arg_keys[8], (NW,), 0, NX * NY), jax.random.fold_in(arg_keys[8], 1), 0, (NX * NY) - 1).astype(jnp.int32)
    agg_map = touch_ends(jax.random.randint(arg_keys[9], (NZ, NX, NY), 0, AGG), jax.random.fold_in(arg_keys[9], 1), 0, AGG - 1).astype(jnp.int32)
    level1_op = draw_level1_op(jax.random.fold_in(arg_keys[12], 71), 0)
    coarsest_inv = draw_coarsest_inv(jax.random.fold_in(arg_keys[12], 71), 0)
    return dict(right_side=right_side, jac_diag=jac_diag, jac_off=jac_off, block_inv=block_inv, press_weight=press_weight, press_diag=press_diag, press_off=press_off, well_index=well_index, well_columns=well_columns, agg_map=agg_map, level1_op=level1_op, coarsest_inv=coarsest_inv)


EPSILON = 1e-06

def neighbours(padded):
    return jnp.stack([padded[..., :-2, 1:-1, 1:-1], padded[..., 2:, 1:-1, 1:-1], padded[..., 1:-1, :-2, 1:-1], padded[..., 1:-1, 2:, 1:-1], padded[..., 1:-1, 1:-1, :-2], padded[..., 1:-1, 1:-1, 2:]])

def layer_apply(field, centre_blocks, side_blocks):
    padded = jnp.pad(field, ((0, 0), (1, 1), (1, 1), (1, 1)))

    def layer(level):
        slab = lax.dynamic_slice_in_dim(padded, level, 3, 1)
        near = neighbours(slab)[:, :, 0]
        centre = slab[:, 1, 1:-1, 1:-1]
        centre_layer = lax.dynamic_index_in_dim(centre_blocks, level, 2, keepdims=False).astype(jnp.float32)
        side_layer = lax.dynamic_index_in_dim(side_blocks, level, 3, keepdims=False).astype(jnp.float32)
        return lax.optimization_barrier(jnp.sum(centre_layer * centre[None], axis=1)) + lax.optimization_barrier(jnp.sum(side_layer * near[:, None], axis=(0, 2)))
    return jnp.moveaxis(lax.map(layer, jnp.arange(NZ, dtype=jnp.int32)), 0, 1)

def block_apply(blocks, field):

    def layer(level):
        block_layer = lax.dynamic_index_in_dim(blocks, level, 2, keepdims=False).astype(jnp.float32)
        field_layer = lax.dynamic_index_in_dim(field, level, 1, keepdims=False)
        return lax.optimization_barrier(jnp.sum(block_layer * field_layer[None], axis=1))
    return jnp.moveaxis(lax.map(layer, jnp.arange(NZ, dtype=jnp.int32)), 0, 1)

def least_squares(hessen, beta):
    upper = [list(line) for line in hessen]
    target = [beta] + [jnp.zeros((), jnp.float32) for line in range(ITERS)]
    rotations = []
    for column in range(ITERS):
        for row, (cosine, sine) in enumerate(rotations):
            first, second = (upper[row][column], upper[row + 1][column])
            upper[row][column] = cosine * first + sine * second
            upper[row + 1][column] = cosine * second - sine * first
        first, second = (upper[column][column], upper[column + 1][column])
        radius = jnp.sqrt(first * first + second * second)
        cosine, sine = (first / radius, second / radius)
        upper[column][column] = radius
        leading = target[column]
        target[column] = cosine * leading
        target[column + 1] = -sine * leading
        rotations.append((cosine, sine))
    weights = [None] * ITERS
    for column in reversed(range(ITERS)):
        total = target[column]
        for later in range(column + 1, ITERS):
            total = total - upper[column][later] * weights[later]
        weights[column] = total / upper[column][column]
    return weights

def reference(right_side, jac_diag, jac_off, block_inv, press_weight, press_diag, press_off, well_index, well_columns, agg_map, level1_op, coarsest_inv):
    columns = jnp.arange(NX * NY, dtype=jnp.int32)
    well_mask = (well_columns[:, None] == columns[None, :]).astype(jnp.float32)
    wells_here = lax.optimization_barrier(jnp.sum(well_mask, axis=0)).reshape(NX, NY)
    well_weight = jnp.dot(well_mask, lax.optimization_barrier(jnp.sum(well_index, axis=0)).reshape(-1), precision=lax.Precision.HIGHEST)

    def well_term(pressure):
        totals = jnp.dot(well_mask, lax.optimization_barrier(jnp.sum(well_index * pressure, axis=0)).reshape(-1), precision=lax.Precision.HIGHEST)
        spread = jnp.dot(totals / well_weight, well_mask, precision=lax.Precision.HIGHEST).reshape(NX, NY)
        return well_index * (wells_here * pressure - spread)

    def apply_fine(field):
        result = layer_apply(field, jac_diag, jac_off)
        return result.at[0].add(well_term(field[0]))

    def apply_column(pressure):
        result = layer_apply(pressure[None], jac_diag[:, 0:1], jac_off[:, :, 0:1])
        return result.at[0].add(well_term(pressure))
    diag_pressure = press_diag.astype(jnp.float32)

    def apply_pressure(field):
        near = neighbours(jnp.pad(field, 1))
        return diag_pressure * field + lax.optimization_barrier(jnp.sum(press_off.astype(jnp.float32) * near, axis=0))
    one_hot = (agg_map[None] == jnp.arange(AGG, dtype=jnp.int32)[:, None, None, None]).astype(jnp.float32)
    coarse_op = level1_op.astype(jnp.float32)
    coarse_diag = jnp.stack([coarse_op[index, index] for index in range(AGG)])

    def precondition(vector):
        pressure_rhs = lax.optimization_barrier(jnp.sum(press_weight.astype(jnp.float32) * vector, axis=0))
        first_guess = pressure_rhs / diag_pressure
        fine_rest = pressure_rhs - apply_pressure(first_guess)
        coarse_rhs = lax.optimization_barrier(jnp.sum((one_hot * fine_rest[None]).reshape(AGG, NZ, NX, NB, BLK), axis=-1))
        coarse_guess = coarse_rhs / coarse_diag
        coarse_rest = coarse_rhs - lax.optimization_barrier(jnp.sum(coarse_op * coarse_guess[None], axis=1))
        coarsest_rhs = lax.optimization_barrier(jnp.sum(coarse_rest, axis=(0, 3))).astype(jnp.bfloat16)
        coarsest = jnp.dot(coarsest_inv.reshape(NZ * NX, NZ * NX), coarsest_rhs.reshape(-1), preferred_element_type=jnp.float32).reshape(NZ, NX)
        coarse_value = coarse_guess + coarsest[None, :, :, None]
        smooth_guess = first_guess + lax.optimization_barrier(jnp.sum(one_hot * jnp.repeat(coarse_value, BLK, axis=-1), axis=0))
        pressure = smooth_guess + (pressure_rhs - apply_pressure(smooth_guess)) / diag_pressure
        remainder = vector - apply_column(pressure)
        correction = block_apply(block_inv, remainder)
        return correction.at[0].add(pressure)
    beta = jnp.sqrt(jnp.sum(right_side * right_side) + EPSILON)
    basis = [right_side / beta]
    directions = []
    hessen = [[jnp.zeros((), jnp.float32) for column in range(ITERS)] for row in range(ITERS + 1)]
    for step in range(ITERS):
        direction = precondition(basis[step])
        image = apply_fine(direction)
        directions.append(direction)
        for row in range(step + 1):
            hessen[row][step] = jnp.sum(image * basis[row])
        rest = image
        for row in range(step + 1):
            rest = rest - hessen[row][step] * basis[row]
        height = jnp.sqrt(jnp.sum(rest * rest) + EPSILON)
        hessen[step + 1][step] = height
        if step + 1 < ITERS:
            basis.append(rest / height)
    weights = least_squares(hessen, beta)
    solution = weights[0] * directions[0]
    for step in range(1, ITERS):
        solution = solution + weights[step] * directions[step]
    residual = right_side - apply_fine(solution)
    hessenberg = jnp.stack([jnp.stack(line) for line in hessen])
    return (solution, residual, hessenberg)
```

```python
import jax
import jax.numpy as jnp
from jax import lax
from jax.experimental import pallas as pl
from jax.experimental.pallas import tpu as pltpu
from jax.sharding import PartitionSpec as P

EPSILON = 1e-06
NC = 12
AGG = 8
F32 = jnp.float32
ROWS, LANES = 8, 128
VMEM = pl.BlockSpec(memory_space=pltpu.VMEM)
SMEM = pl.BlockSpec(memory_space=pltpu.SMEM)


def dense(a):
    s = a.shape[:-2]
    n = len(s)
    a = jnp.swapaxes(a.reshape(s + (2, 4, LANES)), n, n + 1)
    return a.reshape(s + (ROWS, LANES))


def undense(a):
    s = a.shape[:-2]
    n = len(s)
    a = jnp.swapaxes(a.reshape(s + (4, 2, LANES)), n, n + 1)
    return a.reshape(s + (2, 4 * LANES))


def grids():
    return (
        lax.broadcasted_iota(jnp.int32, (ROWS, LANES), 0),
        lax.broadcasted_iota(jnp.int32, (ROWS, LANES), 1),
    )


def even_rows():
    return (grids()[0] & 1) == 0


def turn(a, shift, axis):
    return pltpu.roll(a, shift % a.shape[axis], axis)


def pack_low(f):
    return jnp.where(even_rows(), f[0], turn(f[1], 1, 0))


def pack_high(f):
    return jnp.where(even_rows(), turn(f[0], -1, 0), f[1])


def along_y(f):
    row, lane = grids()
    t = turn(f, 1, 1)
    before = jnp.where(lane == 0, jnp.where(row < 2, 0.0, turn(t, 2, 0)), t)
    t = turn(f, -1, 1)
    after = jnp.where(lane == LANES - 1, jnp.where(row >= ROWS - 2, 0.0, turn(t, -2, 0)), t)
    return before, after


def near(f, zlo, zhi, xlo, xhi):
    even = even_rows()
    y0, y1 = along_y(f[0]), along_y(f[1])
    xm = (
        jnp.where(even, xlo, turn(f[0], 1, 0)),
        jnp.where(even, turn(xlo, -1, 0), turn(f[1], 1, 0)),
    )
    xp = (
        jnp.where(even, turn(f[0], -1, 0), turn(xhi, 1, 0)),
        jnp.where(even, turn(f[1], -1, 0), xhi),
    )
    return ((zlo, f[0]), (f[1], zhi), xm, xp, (y0[0], y1[0]), (y0[1], y1[1]))


def position():
    return lax.axis_index("gz"), lax.axis_index("xy")


def edges(sizes, halos):
    g, s = position()
    ok = (g > 0, g < sizes[0] - 1, s > 0, s < sizes[1] - 1)
    return [jnp.where(o, h, 0.0) for o, h in zip(ok, halos)]


def total(a):
    return jnp.sum(jnp.sum(a, axis=0, keepdims=True), axis=1, keepdims=True)


def scalar_stencil(f, halos, pd, po):
    nb = near(f, *halos)
    out = []
    for z in range(2):
        t = pd[z].astype(F32) * f[z]
        for k in range(6):
            t = t + po[k, z].astype(F32) * nb[k][z]
        out.append(t)
    return out


def call(body, outs, ins, args, **kw):
    return pl.pallas_call(
        body,
        out_shape=[jax.ShapeDtypeStruct(o, F32) for o in outs],
        in_specs=ins,
        out_specs=[VMEM] * len(outs),
        **kw,
    )(*args)


def rings(msgs):
    out = []
    for m, (axis, step) in zip(msgs, (("gz", 1), ("gz", -1), ("xy", 1), ("xy", -1))):
        if m is None:
            continue
        n = lax.axis_size(axis)
        out.append(lax.ppermute(m, axis, [(i, (i + step) % n) for i in range(n)]))
    return out


def spread(buf, axis):
    return lax.all_to_all(buf, axis, 0, 0, tiled=True)


def guess_of(v, pw, pd, rhs_ref, fg_ref):
    fg = []
    for z in range(2):
        t = pw[0, z].astype(F32) * v[0][z]
        for i in range(1, NC):
            t = t + pw[i, z].astype(F32) * v[i][z]
        rhs_ref[z] = t
        fg.append(t / pd[z].astype(F32))
        fg_ref[z] = fg[z]
    return fg


def first_kernel(
    cols, r, pw, pd, wi, inv, rhs_ref, fg_ref, up_z, down_z, up_x, down_x, wc_ref, ws_ref
):
    v = [[r[i, z] for z in range(2)] for i in range(NC)]
    fg = guess_of(v, pw, pd, rhs_ref, fg_ref)
    low, high = pack_low(fg), pack_high(fg)
    rows = [[inv[z, x].astype(F32) for x in range(2)] for z in range(2)]
    for ref, field, pair in (
        (up_z, fg[1], rows[1]),
        (down_z, fg[0], rows[0]),
        (up_x, high, (rows[0][1], rows[1][1])),
        (down_x, low, (rows[0][0], rows[1][0])),
    ):
        ref[0] = field
        for n in range(2):
            for h in range(2):
                ref[1 + 2 * n + h] = jnp.zeros((ROWS, LANES), F32)
                ref[1 + 2 * n + h, :, 0:64] = pair[n][8 * h : 8 * h + 8]
    row, lane = grids()
    _, s = position()
    here = (2 * s + (row & 1)) * 512 + (row >> 1) * LANES + lane
    count = jnp.zeros((ROWS, LANES), F32)
    for w in range(cols.shape[0]):
        count = count + jnp.where(here == cols[w], 1.0, 0.0)
    for z in range(2):
        wc_ref[z] = wi[z] * count
    ws_ref[...] = wi[0] + wi[1]


def coarse_kernel(sizes, extra_is_dots, fg, rhs, zlo, zhi, xlo, xhi, pd, po, ag, lv, extra, part_ref,
                  up_z, down_z, up_x, down_x, buf):
    halos = edges(sizes, [h[0] for h in (zlo, zhi, xlo, xhi)])
    f = [fg[0], fg[1]]
    applied = scalar_stencil(f, halos, pd, po)
    row16 = lax.broadcasted_iota(jnp.int32, (16, LANES), 0)
    lane16 = lax.broadcasted_iota(jnp.int32, (16, LANES), 1)
    even = (lax.broadcasted_iota(jnp.int32, (ROWS, 1), 0) & 1) == 0
    g, s = position()
    tile = jnp.zeros((16, LANES), F32)
    part = []
    for z in range(2):
        rest = rhs[z] - applied[z]
        level = lv[z]
        guess = f[z]
        sums = jnp.zeros((ROWS, 1), F32)
        for a in range(AGG):
            mine = ag[z] == a
            c = jnp.sum(jnp.where(mine, rest, 0.0), axis=1, keepdims=True)
            value = c / level[:, a : a + 1]
            guess = guess + jnp.where(mine, value, 0.0)
            sums = sums + (c - level[:, AGG + a : AGG + a + 1] * value)
        part.append(guess)
        part_ref[z] = guess
        for x in range(2):
            t = jnp.sum(jnp.where(even if x == 0 else ~even, sums, 0.0), axis=0, keepdims=True)
            tile = tile + jnp.where((row16 == 2 * g + z) & (lane16 == 2 * s + x), t, 0.0)
    up_z[...] = part[1]
    down_z[...] = part[0]
    up_x[...] = pack_high(part)
    down_x[...] = pack_low(part)
    top = tile[0:8] + extra[...] if extra_is_dots else tile[0:8]
    for m in range(buf.shape[0]):
        buf[m, 0] = top
        buf[m, 1] = tile[8:16]
        if not extra_is_dots:
            buf[m, 2] = extra[...]


def relay_kernel(n, got, *outs):
    size, parts = got.shape[0], got.shape[1]
    sums = []
    for q in range(parts):
        t = got[0, q]
        for m in range(1, size):
            t = t + got[m, q]
        sums.append(t)
    for m in range(outs[0].shape[0]):
        for q in range(n):
            outs[0][m, q] = sums[q]
    if len(outs) > 1:
        outs[1][...] = sums[n]


def pressure_kernel(sizes, got, inv, nz, pz, nx, px, part, hzlo, hzhi, hxlo, hxhi, rhs, pd, po, wi,
                    p_ref, buf, up_x, down_x, tops_ref):
    even = even_rows()
    t = [got[0, q] for q in range(2)]
    for m in range(1, got.shape[0]):
        t = [t[q] + got[m, q] for q in range(2)]
    tops_ref[...] = t[0]
    a, b = t[0][:, 0:64], t[1][:, 0:64]

    def beside(ref):
        return [total(ref[1 + 2 * n, :, 0:64] * a + ref[2 + 2 * n, :, 0:64] * b) for n in range(2)]

    own = []
    for z in range(2):
        pair = []
        for x in range(2):
            w = inv[z, x].astype(F32)
            pair.append(total(w[0:8] * a + w[8:16] * b))
        own.append(jnp.where(even, pair[0], pair[1]))
    halos = []
    for ref, h in ((nz, hzlo), (pz, hzhi), (nx, hxlo), (px, hxhi)):
        c = beside(ref)
        halos.append(h[...] + jnp.where(even, c[0], c[1]))
    halos = edges(sizes, halos)
    f = [part[z] + own[z] for z in range(2)]
    applied = scalar_stencil(f, halos, pd, po)
    p = []
    for z in range(2):
        p.append(f[z] + (rhs[z] - applied[z]) / pd[z].astype(F32))
        p_ref[z] = p[z]
    up_x[...] = pack_high(p)
    down_x[...] = pack_low(p)
    column = wi[0] * p[0] + wi[1] * p[1]
    for m in range(buf.shape[0]):
        buf[m, 0] = p[0]
        buf[m, 1] = p[1]
        buf[m, 2] = column


def columns_of(got, q):
    t = got[0, q]
    for m in range(1, got.shape[0]):
        t = t + got[m, q]
    return t


def steps_of(tops):
    rr, rw, ww = (total(tops[0:1, 64 + m : 65 + m]) for m in range(3))
    beta = jnp.sqrt(rr + EPSILON)
    h00 = rw / (beta * beta)
    rest = jnp.maximum(ww / (beta * beta) - h00 * h00, 0.0)
    return beta, h00, jnp.sqrt(rest + EPSILON)


def direction_kernel(sizes, later, v, p, got, hxlo, hxhi, jd, jo, bi, wc, wsum, wi, tops, d0,
                     d_ref, up_z, down_z, up_x, down_x, buf):
    g, _ = position()
    f = [p[0], p[1]]
    halos = edges(
        sizes,
        [got[jnp.maximum(g - 1, 0), 1], got[jnp.minimum(g + 1, sizes[0] - 1), 0], hxlo[...], hxhi[...]],
    )
    nb = near(f, *halos)
    level = columns_of(got, 2) / wsum[...]
    rem = []
    for i in range(NC):
        pair = []
        for z in range(2):
            t = jd[i, z].astype(F32) * f[z]
            for k in range(6):
                t = t + jo[k, i, z].astype(F32) * nb[k][z]
            if i == 0:
                t = t + wc[z] * (f[z] - level)
            pair.append(v[i, z] - t)
        rem.append(pair)
    if later:
        beta, h00, h10 = steps_of(tops)
        scale = 1.0 / (beta * h10)
    for i in range(NC):
        pair = []
        for z in range(2):
            ts = [None, None]
            for j in range(NC):
                u = bi[i, j, z].astype(F32) * rem[j][z]
                ts[j % 2] = u if ts[j % 2] is None else ts[j % 2] + u
            t = ts[0] + ts[1]
            if i == 0:
                t = t + f[z]
            if later:
                t = (t - h00 * d0[i, z]) * scale
            d_ref[i, z] = t
            pair.append(t)
        up_z[i] = pair[1]
        down_z[i] = pair[0]
        up_x[i] = pack_high(pair)
        down_x[i] = pack_low(pair)
        if i == 0:
            column = wi[0] * pair[0] + wi[1] * pair[1]
            for m in range(buf.shape[0]):
                buf[m, 0] = column


def image_kernel(sizes, later, d, zlo, zhi, xlo, xhi, got, jd, jo, wc, wsum, r, w0, tops, pw, pd,
                 w_ref, dots_ref, *more):
    *outs, nb = more
    level = columns_of(got, 0) / wsum[...]
    for j in range(NC):
        f = [d[j, 0], d[j, 1]]
        n = near(f, *edges(sizes, [h[j] for h in (zlo, zhi, xlo, xhi)]))
        for z in range(2):
            nb[0, j, z] = f[z]
            for k in range(6):
                nb[k + 1, j, z] = n[k][z]

    def row(i, carry):
        for z in range(2):
            ts = [None] * 4
            for k in range(7):
                for j in range(NC):
                    c = (jd[i, j, z] if k == 0 else jo[k - 1, i, j, z]).astype(F32)
                    u = c * nb[k, j, z]
                    q = j % 4
                    ts[q] = u if ts[q] is None else ts[q] + u
            w_ref[i, z] = (ts[0] + ts[1]) + (ts[2] + ts[3])
        return carry

    lax.fori_loop(0, NC, row, 0)
    for z in range(2):
        w_ref[0, z] = w_ref[0, z] + wc[z] * (d[0, z] - level)
    if later:
        beta, h00, h10 = steps_of(tops)
        scale = 1.0 / (beta * h10)
    sums = [jnp.zeros((ROWS, LANES), F32) for _ in range(3)]
    for i in range(NC):
        for z in range(2):
            w = w_ref[i, z]
            if later:
                first = w * (r[i, z] * (1.0 / beta))
                second = w * ((w0[i, z] - h00 * r[i, z]) * scale)
            else:
                first = r[i, z] * r[i, z]
                second = w * r[i, z]
            sums = [sums[0] + first, sums[1] + second, sums[2] + w * w]
    row_at, lane = grids()
    t = jnp.zeros((ROWS, LANES), F32)
    for m in range(3):
        t = t + jnp.where((row_at == 0) & (lane == 64 + m), total(sums[m]), 0.0)
    if later:
        for m in range(dots_ref.shape[0]):
            dots_ref[m, 0] = t
    else:
        dots_ref[...] = t
        rhs_ref, fg_ref, up_z, down_z, up_x, down_x = outs
        v = [[w_ref[i, z] for z in range(2)] for i in range(NC)]
        fg = guess_of(v, pw, pd, rhs_ref, fg_ref)
        up_z[0] = fg[1]
        down_z[0] = fg[0]
        up_x[0] = pack_high(fg)
        down_x[0] = pack_low(fg)


def last_kernel(got, tops, r, d0, w0, d1, w1, sol_ref, res_ref, hess_ref):
    t = got[0, 0]
    for m in range(1, got.shape[0]):
        t = t + got[m, 0]
    h01, h11, norm = (total(t[0:1, 64 + m : 65 + m]) for m in range(3))
    beta, h00, h10 = steps_of(tops)
    h21 = jnp.sqrt(jnp.maximum(norm - h01 * h01 - h11 * h11, 0.0) + EPSILON)
    radius = jnp.sqrt(h00 * h00 + h10 * h10)
    c0, s0 = h00 / radius, h10 / radius
    u00, u01, u11 = radius, c0 * h01 + s0 * h11, c0 * h11 - s0 * h01
    t0, t1 = c0 * beta, -s0 * beta
    radius = jnp.sqrt(u11 * u11 + h21 * h21)
    t1 = (u11 / radius) * t1
    y1 = t1 / radius
    y0 = (t0 - u01 * y1) / u00
    y0 = y0 / beta
    for i in range(NC):
        for z in range(2):
            sol_ref[i, z] = y0 * d0[i, z] + y1 * d1[i, z]
            res_ref[i, z] = r[i, z] - (y0 * w0[i, z] + y1 * w1[i, z])
    at = lax.broadcasted_iota(jnp.int32, (3, 2), 0)
    col = lax.broadcasted_iota(jnp.int32, (3, 2), 1)
    h = jnp.zeros((3, 2), F32)
    for i, j, value in ((0, 0, h00), (1, 0, h10), (0, 1, h01), (1, 1, h11), (2, 1, h21)):
        h = h + jnp.where((at == i) & (col == j), value, 0.0)
    hess_ref[...] = h


def on_device(
    right_side, jac_diag, jac_off, block_inv, press_weight, press_diag, press_off, well_index,
    well_columns, agg_map, level1_op, coarsest_inv,
):
    sizes = (lax.axis_size("gz"), lax.axis_size("xy"))
    r, jd, jo, bi = dense(right_side), dense(jac_diag), dense(jac_off), dense(block_inv)
    pw, pd, po = dense(press_weight), dense(press_diag), dense(press_off)
    wi, ag = dense(well_index), dense(agg_map)
    op = level1_op.astype(F32)
    lv = jnp.concatenate([jnp.stack([op[a, a] for a in range(AGG)]), jnp.sum(op, axis=0)])
    lv = lv.transpose(1, 3, 2, 0).reshape(2, ROWS, 2 * AGG)
    vec, field, plane, msg = (NC, 2, ROWS, LANES), (2, ROWS, LANES), (ROWS, LANES), (5, ROWS, LANES)
    side = (NC, ROWS, LANES)
    gz, xy = sizes
    jd0, jo0 = jd[:, 0], jo[:, :, 0]

    def bind(body, *static):
        def kernel(*refs):
            return body(*static, *refs)

        return kernel

    rhs, fg, *msgs, wc, ws = call(
        first_kernel, [field, field, msg, msg, msg, msg, field, plane], [SMEM] + [VMEM] * 5,
        (well_columns, r, pw, pd, wi, coarsest_inv),
    )
    v, extra, rows, wsum = r, ws, None, None
    kept = []
    for step in range(2):
        later = step == 1
        halo = rings(msgs)
        rows = halo if rows is None else rows
        parts = 2 if later else 3
        part, *msgs, buf = call(
            bind(coarse_kernel, sizes, later), [field] + [plane] * 4 + [(gz, parts, ROWS, LANES)],
            [VMEM] * 11, (fg, rhs, *halo, pd, po, ag, lv, extra),
        )
        halo = rings(msgs)
        got = spread(buf, "gz")
        outs = [(xy, 2, ROWS, LANES)] + ([] if later else [plane])
        buf, *found = call(bind(relay_kernel, 2), outs, [VMEM], (got,))
        wsum = found[0] if found else wsum
        got = spread(buf, "xy")
        p, buf, *msgs, tops = call(
            bind(pressure_kernel, sizes), [field, (gz, 3, ROWS, LANES), plane, plane, plane],
            [VMEM] * 15, (got, coarsest_inv, *rows, part, *halo, rhs, pd, po, wi),
        )
        xlo, xhi = rings([None, None, *msgs])
        got = spread(buf, "gz")
        d0 = kept[0][0] if later else r
        d, *msgs, buf = call(
            bind(direction_kernel, sizes, later), [vec, side, side, side, side, (gz, 1, ROWS, LANES)],
            [VMEM] * 13,
            (v, p, got, xlo, xhi, jd0, jo0, bi, wc, wsum, wi, tops, d0),
        )
        halo = rings(msgs)
        got = spread(buf, "gz")
        outs = [vec, (gz, 1, ROWS, LANES)] if later else [vec, plane, field, field] + [(1, *plane)] * 4
        w0 = kept[0][1] if later else r
        w, dots, *more = call(
            bind(image_kernel, sizes, later), outs, [VMEM] * 15,
            (d, *halo, got, jd, jo, wc, wsum, r, w0, tops, pw, pd),
            scratch_shapes=[pltpu.VMEM((7, NC, 2, ROWS, LANES), F32)],
        )
        kept.append((d, w))
        if not later:
            rhs, fg, *msgs = more
            v, extra = w, dots
    got = spread(dots, "gz")
    (buf,) = call(bind(relay_kernel, 1), [(xy, 1, ROWS, LANES)], [VMEM], (got,))
    got = spread(buf, "xy")
    solution, residual, hessenberg = call(
        last_kernel, [vec, vec, (3, 2)], [VMEM] * 7, (got, tops, r, *kept[0], *kept[1])
    )
    return undense(solution), undense(residual), hessenberg


def solution(mesh):
    return jax.shard_map(
        on_device,
        mesh=mesh,
        in_specs=(
            P(None, "gz", "xy", None),
            P(None, None, "gz", "xy", None),
            P(None, None, None, "gz", "xy", None),
            P(None, None, "gz", "xy", None),
            P(None, "gz", "xy", None),
            P("gz", "xy", None),
            P(None, "gz", "xy", None),
            P("gz", "xy", None),
            P(),
            P("gz", "xy", None),
            P(None, None, "gz", "xy", None),
            P("gz", "xy", None, None),
        ),
        out_specs=(P(None, "gz", "xy", None), P(None, "gz", "xy", None), P()),
        check_vma=False,
    )
```

```python
import jax
import jax.numpy as jnp
from jax import lax
from jax.experimental import pallas as pl
from jax.experimental.pallas import tpu as pltpu
from jax.sharding import PartitionSpec as P

EPSILON = 1e-06
NC = 12
AGG = 8
F32 = jnp.float32
ROWS, LANES = 8, 128
VMEM = pl.BlockSpec(memory_space=pltpu.VMEM)
SMEM = pl.BlockSpec(memory_space=pltpu.SMEM)


def dense(a):
    s = a.shape[:-2]
    n = len(s)
    a = jnp.swapaxes(a.reshape(s + (2, 4, LANES)), n, n + 1)
    return a.reshape(s + (ROWS, LANES))


def undense(a):
    s = a.shape[:-2]
    n = len(s)
    a = jnp.swapaxes(a.reshape(s + (4, 2, LANES)), n, n + 1)
    return a.reshape(s + (2, 4 * LANES))


def grids():
    return (
        lax.broadcasted_iota(jnp.int32, (ROWS, LANES), 0),
        lax.broadcasted_iota(jnp.int32, (ROWS, LANES), 1),
    )


def even_rows():
    return (grids()[0] & 1) == 0


def turn(a, shift, axis):
    return pltpu.roll(a, shift % a.shape[axis], axis)


def pack_low(f):
    return jnp.where(even_rows(), f[0], turn(f[1], 1, 0))


def pack_high(f):
    return jnp.where(even_rows(), turn(f[0], -1, 0), f[1])


def along_y(f):
    row, lane = grids()
    t = turn(f, 1, 1)
    before = jnp.where(lane == 0, jnp.where(row < 2, 0.0, turn(t, 2, 0)), t)
    t = turn(f, -1, 1)
    after = jnp.where(lane == LANES - 1, jnp.where(row >= ROWS - 2, 0.0, turn(t, -2, 0)), t)
    return before, after


def near(f, zlo, zhi, xlo, xhi):
    even = even_rows()
    y0, y1 = along_y(f[0]), along_y(f[1])
    xm = (
        jnp.where(even, xlo, turn(f[0], 1, 0)),
        jnp.where(even, turn(xlo, -1, 0), turn(f[1], 1, 0)),
    )
    xp = (
        jnp.where(even, turn(f[0], -1, 0), turn(xhi, 1, 0)),
        jnp.where(even, turn(f[1], -1, 0), xhi),
    )
    return ((zlo, f[0]), (f[1], zhi), xm, xp, (y0[0], y1[0]), (y0[1], y1[1]))


def position():
    return lax.axis_index("gz"), lax.axis_index("xy")


def edges(sizes, halos):
    g, s = position()
    ok = (g > 0, g < sizes[0] - 1, s > 0, s < sizes[1] - 1)
    return [jnp.where(o, h, 0.0) for o, h in zip(ok, halos)]


def total(a):
    return jnp.sum(jnp.sum(a, axis=0, keepdims=True), axis=1, keepdims=True)


def scalar_stencil(f, halos, pd, po):
    nb = near(f, *halos)
    out = []
    for z in range(2):
        t = pd[z].astype(F32) * f[z]
        for k in range(6):
            t = t + po[k, z].astype(F32) * nb[k][z]
        out.append(t)
    return out


def summed(got, q):
    t = got[0, q]
    for m in range(1, got.shape[0]):
        t = t + got[m, q]
    return t


def beside_z(sizes, got, q, below):
    g, _ = position()
    return got[jnp.maximum(g - 1, 0) if below else jnp.minimum(g + 1, sizes[0] - 1), q]


def packed(levels):
    return pack_high([levels[0]] * 2), pack_low([levels[1]] * 2)


def call(body, outs, ins, args, fast=True, **kw):
    return pl.pallas_call(
        body,
        out_shape=[pltpu.VMEM(o, F32) if fast else jax.ShapeDtypeStruct(o, F32) for o in outs],
        in_specs=ins,
        out_specs=[VMEM] * len(outs),
        **kw,
    )(*args)


def near_by(a):
    return pltpu.with_memory_space_constraint(a, pltpu.VMEM)


def rings(msgs):
    out = []
    for m, (axis, step) in zip(msgs, (("gz", 1), ("gz", -1), ("xy", 1), ("xy", -1))):
        if m is None:
            continue
        n = lax.axis_size(axis)
        out.append(near_by(lax.ppermute(m, axis, [(i, (i + step) % n) for i in range(n)])))
    return out


def spread(buf, axis, shape=None):
    got = lax.all_to_all(buf, axis, 0, 0, tiled=True)
    return near_by(got if shape is None else got.reshape(shape))


def guess_of(v, pw, pd, rhs_ref, fg_ref):
    fg = []
    for z in range(2):
        t = pw[0, z].astype(F32) * v[0][z]
        for i in range(1, NC):
            t = t + pw[i, z].astype(F32) * v[i][z]
        rhs_ref[z] = t
        fg.append(t / pd[z].astype(F32))
        fg_ref[z] = fg[z]
    return fg


def order_inverse(inv, inv_ref):
    col = lax.broadcasted_iota(jnp.int32, (64, LANES), 0)
    lane = lax.broadcasted_iota(jnp.int32, (64, LANES), 1)
    wanted = 2 * (lane >> 5) + (lane & 1)
    mine = (col & 15) == ((lane & 31) >> 1)
    for m in range(ROWS):
        pick = jnp.where(col == 8 * m + wanted, 1.0, 0.0).astype(jnp.bfloat16)
        t = jnp.dot(inv[...], pick, preferred_element_type=F32)
        t = jnp.where(mine, t, 0.0)
        for n in range(4):
            inv_ref[n, m : m + 1, :] = jnp.sum(t[16 * n : 16 * n + 16], axis=0, keepdims=True)


def in_one_row(values):
    return jnp.sum(pltpu.roll(values, 0, 1, stride=16, stride_axis=0), axis=0, keepdims=True)


def in_rows(row):
    at, _ = grids()
    t = jnp.broadcast_to(row, (ROWS, LANES))
    for bit in (1, 2, 4):
        t = jnp.where((at & bit) != 0, turn(t, -16 * bit, 1), t)
    return t


def two_rows(ref, first, second):
    at = lax.broadcasted_iota(jnp.int32, ref.shape, 0)
    ref[...] = jnp.where((at & 1) == 0, first, second)


GUESS, INVERSE, AGGREGATE, SHARE, WEIGHT = 0, 1, 3, 4, 5


def first_kernel(
    cols, r, pw, pd, wi, ag, inv, rhs_ref, fg_ref, up_z, down_z, up_x, down_x, wc_ref, inv_ref
):
    v = [[r[i, z] for z in range(2)] for i in range(NC)]
    fg = guess_of(v, pw, pd, rhs_ref, fg_ref)
    order_inverse(inv, inv_ref)
    row, lane = grids()
    _, s = position()
    here = (2 * s + (row & 1)) * 512 + (row >> 1) * LANES + lane
    count = jnp.zeros((ROWS, LANES), F32)
    for w in range(cols.shape[0]):
        count = count + jnp.where(here == cols[w], 1.0, 0.0)
    wc = [wi[z] * count for z in range(2)]
    for z in range(2):
        wc_ref[z] = wc[z]
    share = [pw[0, z].astype(F32) * wc[z] / pd[z].astype(F32) for z in range(2)]
    agg = [ag[z].astype(F32) for z in range(2)]
    weight = wi[0] + wi[1]
    for ref, pick, pair in (
        (up_z, lambda f: f[1], (2, 3)),
        (down_z, lambda f: f[0], (0, 1)),
        (up_x, pack_high, (1, 3)),
        (down_x, pack_low, (0, 2)),
    ):
        ref[GUESS] = pick(fg)
        for n in range(2):
            ref[INVERSE + n] = inv_ref[pair[n]]
        ref[AGGREGATE] = pick(agg)
        ref[SHARE] = pick(share)
        ref[WEIGHT] = weight


def coarse_body(fg, rhs, halos, pd, po, ag, lv, part_ref):
    applied = scalar_stencil(fg, halos, pd, po)
    _, lane = grids()
    even = (lax.broadcasted_iota(jnp.int32, (ROWS, 1), 0) & 1) == 0
    g, s = position()
    place = 32 * (s & 3) + 4 * g
    tile = jnp.zeros((1, LANES), F32)
    at = lax.broadcasted_iota(jnp.int32, (1, LANES), 1)
    values = jnp.zeros((ROWS, LANES), F32)
    for z in range(2):
        rest = rhs[z] - applied[z]
        level = lv[z]
        guess = fg[z]
        sums = jnp.zeros((ROWS, 1), F32)
        for a in range(AGG):
            mine = ag[z] == a
            c = jnp.sum(jnp.where(mine, rest, 0.0), axis=1, keepdims=True)
            value = c / level[:, a : a + 1]
            guess = guess + jnp.where(mine, value, 0.0)
            sums = sums + (c - level[:, AGG + a : AGG + a + 1] * value)
            values = values + jnp.where(lane == AGG * z + a, value, 0.0)
        part_ref[z] = guess
        for x in range(2):
            t = jnp.sum(jnp.where(even if x == 0 else ~even, sums, 0.0), axis=0, keepdims=True)
            tile = tile + jnp.where(at == place + 2 * z + x, t, 0.0)
    return tile, in_one_row(values)


def first_coarse_kernel(sizes, fg, rhs, wi, zlo, zhi, xlo, xhi, pd, po, ag, lv, part_ref, rows_ref, buf):
    halos = edges(sizes, [h[GUESS] for h in (zlo, zhi, xlo, xhi)])
    tile, values = coarse_body([fg[0], fg[1]], rhs, halos, pd, po, ag, lv, part_ref)
    two_rows(rows_ref, tile, values)
    weight = wi[0] + wi[1]
    for m in range(buf.shape[0]):
        buf[m, 0] = rows_ref[0:ROWS]
        buf[m, 1] = weight
        buf[m, 2] = xlo[WEIGHT]
        buf[m, 3] = xhi[WEIGHT]


def second_coarse_kernel(
    sizes, fg, rhs, r, w, wc, pw, wsums, got, xlo, xhi, szlo, szhi, sxlo, sxhi, dots, pd, po, ag, lv,
    part_ref, rhs_ref, halo_ref, level_ref, rows_ref,
):
    level = summed(got, 1) / wsums[0]
    level_ref[...] = level
    sides = packed([summed(got, 2) / wsums[1], summed(got, 3) / wsums[2]])
    halos = [
        beside_z(sizes, got, 0, True) - szlo[SHARE] * level,
        beside_z(sizes, got, 0, False) - szhi[SHARE] * level,
        xlo[...] - sxlo[SHARE] * sides[0],
        xhi[...] - sxhi[SHARE] * sides[1],
    ]
    halos = edges(sizes, halos)
    for n in range(4):
        halo_ref[n] = halos[n]
    rhs_now, fg_now = [], []
    first = second = jnp.zeros((ROWS, LANES), F32)
    for z in range(2):
        fall = wc[z] * level
        t = rhs[z] - pw[0, z].astype(F32) * fall
        rhs_ref[z] = t
        rhs_now.append(t)
        fg_now.append(t / pd[z].astype(F32))
        first = first + r[0, z] * fall
        second = second + (2.0 * w[0, z] - fall) * fall
    tile, values = coarse_body(fg_now, rhs_now, halos, pd, po, ag, lv, part_ref)
    _, s = position()
    lane = lax.broadcasted_iota(jnp.int32, (1, LANES), 1)
    sums = dots[0:1]
    for m, t in ((1, first), (2, second)):
        sums = sums - jnp.where(lane == m, total(t), 0.0)
    two_rows(rows_ref, tile + pltpu.roll(sums, 32 * ((s + 1) & 3), 1), values)


def relay(rows, own, out_ref):
    at = lax.broadcasted_iota(jnp.int32, rows.shape, 0)
    tile = jnp.sum(jnp.where((at & 1) == 0, rows, 0.0), axis=0, keepdims=True)
    two_rows(out_ref, tile, own)


def first_relay_kernel(got, own, out_ref, sums_ref, rows_ref):
    for m in range(got.shape[0]):
        rows_ref[2 * m : 2 * m + 2] = got[m, 0, 0:2]
    relay(rows_ref[...], own[1:2], out_ref)
    for n in range(3):
        sums_ref[n] = summed(got, 1 + n)


def second_relay_kernel(got, own, out_ref):
    relay(got[...], own[1:2], out_ref)


def pressure_kernel(sizes, later, got, got_z, inv, zlo, zhi, xlo, xhi, halo, part, rhs, pd, po, wi,
                    p_ref, buf, up_x, down_x, tops_ref):
    even = even_rows()
    _, s = position()
    g, _ = position()
    _, lane = grids()
    t = tops = jnp.zeros((ROWS, LANES), F32)
    for k in range(4):
        some = got[pl.ds(2 * k, ROWS, stride=8), :]
        t = t + jnp.where((lane >> 5) == k, some, 0.0)
        tops = tops + turn(some, -32 * ((k + 1) % 4), 1)
    tops_ref[...] = tops
    own = []
    for z in range(2):
        pair = [total(inv[2 * z + x] * t) for x in range(2)]
        own.append(jnp.where(even, pair[0], pair[1]))
    low = in_rows(got[pl.ds(2 * jnp.maximum(s - 1, 0) + 1, 1), :])
    high = in_rows(got[pl.ds(2 * jnp.minimum(s + 1, sizes[1] - 1) + 1, 1), :])
    below = in_rows(got_z[pl.ds(2 * jnp.maximum(g - 1, 0) + 1, 1), :])
    above = in_rows(got_z[pl.ds(2 * jnp.minimum(g + 1, sizes[0] - 1) + 1, 1), :])
    low_even, high_odd = turn(low, -1, 0), turn(high, 1, 0)
    halos = []
    for n, ref in enumerate((zlo, zhi, xlo, xhi)):
        c = [total(ref[INVERSE + m] * t) for m in range(2)]
        h = halo[n] if later else ref[GUESS]
        h = h + jnp.where(even, c[0], c[1])
        agg = ref[AGGREGATE]
        for a in range(AGG):
            one, two = slice(a, a + 1), slice(AGG + a, AGG + a + 1)
            value = (
                below[:, two],
                above[:, one],
                jnp.where(even, low_even[:, one], low[:, two]),
                jnp.where(even, high[:, one], high_odd[:, two]),
            )[n]
            h = h + jnp.where(agg == float(a), value, 0.0)
        halos.append(h)
    halos = edges(sizes, halos)
    f = [part[z] + own[z] for z in range(2)]
    applied = scalar_stencil(f, halos, pd, po)
    p = []
    for z in range(2):
        p.append(f[z] + (rhs[z] - applied[z]) / pd[z].astype(F32))
        p_ref[z] = p[z]
    up_x[...] = pack_high(p)
    down_x[...] = pack_low(p)
    column = wi[0] * p[0] + wi[1] * p[1]
    for m in range(buf.shape[0]):
        buf[m, 0] = jnp.where(g < m, p[1], p[0])
        buf[m, 1] = column


def steps_of(tops):
    rr, rw, ww = (total(tops[:, m : m + 1]) for m in range(3))
    beta = jnp.sqrt(rr + EPSILON)
    h00 = rw / (beta * beta)
    rest = jnp.maximum(ww / (beta * beta) - h00 * h00, 0.0)
    return beta, h00, jnp.sqrt(rest + EPSILON)


def direction_kernel(sizes, later, v, p, got, hxlo, hxhi, jd, jo, bi, wc, wsums, wi, *more):
    if later:
        tops, d0, old, *more = more
        beta, h00, h10 = steps_of(tops)
        scale = 1.0 / (beta * h10)
    d_ref, up_z, down_z, up_x, down_x, column_ref = more
    f = [p[0], p[1]]
    halos = [beside_z(sizes, got, 0, True), beside_z(sizes, got, 0, False), hxlo[...], hxhi[...]]
    nb = near(f, *edges(sizes, halos))
    level = summed(got, 1) / wsums[0]
    rem = []
    for i in range(NC):
        pair = []
        for z in range(2):
            t = jd[i, z].astype(F32) * f[z]
            for k in range(6):
                t = t + jo[k, i, z].astype(F32) * nb[k][z]
            if i == 0:
                t = t + wc[z] * (f[z] - level)
                if later:
                    t = t + wc[z] * old[...]
            pair.append(v[i, z] - t)
        rem.append(pair)
    for i in range(NC):
        pair = []
        for z in range(2):
            ts = [None, None]
            for j in range(NC):
                u = bi[i, j, z].astype(F32) * rem[j][z]
                ts[j % 2] = u if ts[j % 2] is None else ts[j % 2] + u
            t = ts[0] + ts[1]
            if i == 0:
                t = t + f[z]
            if later:
                t = (t - h00 * d0[i, z]) * scale
            d_ref[i, z] = t
            pair.append(t)
        up_z[i] = pair[1]
        down_z[i] = pair[0]
        up_x[i] = pack_high(pair)
        down_x[i] = pack_low(pair)
        if i == 0:
            column = wi[0] * pair[0] + wi[1] * pair[1]
            column_ref[...] = column
            if not later:
                up_x[NC] = column
                down_x[NC] = column


def image_kernel(sizes, later, d, zlo, zhi, xlo, xhi, column, jd, jo, wc, r, *more):
    if later:
        w0, tops, old, w_ref, buf, nb = more
    else:
        pw, pd, w_ref, buf, rhs_ref, fg_ref, up_x, down_x, dots_ref, nb = more
    for j in range(NC):
        f = [d[j, 0], d[j, 1]]
        n = near(f, *edges(sizes, [h[j] for h in (zlo, zhi, xlo, xhi)]))
        for z in range(2):
            nb[0, j, z] = f[z]
            for k in range(6):
                nb[k + 1, j, z] = n[k][z]

    def row(i, carry):
        for z in range(2):
            ts = [None] * 4
            for k in range(7):
                for j in range(NC):
                    c = (jd[i, j, z] if k == 0 else jo[k - 1, i, j, z]).astype(F32)
                    u = c * nb[k, j, z]
                    q = j % 4
                    ts[q] = u if ts[q] is None else ts[q] + u
            w_ref[i, z] = (ts[0] + ts[1]) + (ts[2] + ts[3])
        return carry

    lax.fori_loop(0, NC, row, 0)
    for z in range(2):
        w_ref[0, z] = w_ref[0, z] + wc[z] * d[0, z]
    row_at, lane = grids()
    zero = jnp.zeros((ROWS, LANES), F32)
    sums = [zero, zero, zero]
    falls = [zero] * 4
    if later:
        beta, h00, h10 = steps_of(tops)
        scale = 1.0 / (beta * h10)
    for i in range(NC):
        for z in range(2):
            w = w_ref[i, z]
            if later:
                before = w0[i, z] - wc[z] * old[...] if i == 0 else w0[i, z]
                b0 = r[i, z] * (1.0 / beta)
                b1 = (before - h00 * r[i, z]) * scale
                first, second = w * b0, w * b1
                if i == 0:
                    falls = [t + wc[z] * u for t, u in zip(falls, (b0, b1, w, wc[z]))]
            else:
                first, second = r[i, z] * r[i, z], w * r[i, z]
            sums = [sums[0] + first, sums[1] + second, sums[2] + w * w]
    t = zero
    for m in range(3):
        t = t + jnp.where((row_at == 0) & (lane == m), total(sums[m]), 0.0)
    if later:
        for m in range(buf.shape[0]):
            buf[m, 0] = t
            buf[m, 1] = column[...]
            for n in range(4):
                buf[m, 2 + n] = falls[n]
    else:
        dots_ref[...] = t
        v = [[w_ref[i, z] for z in range(2)] for i in range(NC)]
        fg = guess_of(v, pw, pd, rhs_ref, fg_ref)
        up_x[...] = pack_high(fg)
        down_x[...] = pack_low(fg)
        below, above = edges(sizes, [zero, zero, xlo[NC], xhi[NC]])[2:]
        g, _ = position()
        for m in range(buf.shape[0]):
            buf[m, 0] = jnp.where(g < m, fg[1], fg[0])
            buf[m, 1] = column[...]
            buf[m, 2] = below
            buf[m, 3] = above


def close_kernel(got, wsums, buf, level_ref):
    row, lane = grids()
    level = summed(got, 1) / wsums[0]
    level_ref[...] = level
    falls = [summed(got, 2 + n) for n in range(4)]
    t = summed(got, 0)
    for m, fall in enumerate((falls[0], falls[1], 2.0 * falls[2] - falls[3] * level)):
        t = t - jnp.where((row == 0) & (lane == m), total(fall * level), 0.0)
    buf[...] = jnp.broadcast_to(t[0:1], buf.shape)


def last_kernel(got, tops, r, d0, w0, d1, w1, wc, level0, level1, sol_ref, res_ref, hess_ref):
    t = jnp.sum(got[...], axis=0, keepdims=True)
    h01, h11, norm = (t[:, m : m + 1] for m in range(3))
    beta, h00, h10 = steps_of(tops)
    h21 = jnp.sqrt(jnp.maximum(norm - h01 * h01 - h11 * h11, 0.0) + EPSILON)
    radius = jnp.sqrt(h00 * h00 + h10 * h10)
    c0, s0 = h00 / radius, h10 / radius
    u00, u01, u11 = radius, c0 * h01 + s0 * h11, c0 * h11 - s0 * h01
    t0, t1 = c0 * beta, -s0 * beta
    radius = jnp.sqrt(u11 * u11 + h21 * h21)
    t1 = (u11 / radius) * t1
    y1 = t1 / radius
    y0 = (t0 - u01 * y1) / u00
    y0 = y0 / beta
    for i in range(NC):
        for z in range(2):
            sol_ref[i, z] = y0 * d0[i, z] + y1 * d1[i, z]
            t = y0 * w0[i, z] + y1 * w1[i, z]
            if i == 0:
                t = t - wc[z] * (y0 * level0[...] + y1 * level1[...])
            res_ref[i, z] = r[i, z] - t
    col = lax.broadcasted_iota(jnp.int32, (2, 3), 0)
    at = lax.broadcasted_iota(jnp.int32, (2, 3), 1)
    h = jnp.zeros((2, 3), F32)
    for i, j, value in ((0, 0, h00), (1, 0, h10), (0, 1, h01), (1, 1, h11), (2, 1, h21)):
        h = h + jnp.where((at == i) & (col == j), value, 0.0)
    hess_ref[...] = h


def on_device(
    right_side, jac_diag, jac_off, block_inv, press_weight, press_diag, press_off, well_index,
    well_columns, agg_map, level1_op, coarsest_inv,
):
    sizes = (lax.axis_size("gz"), lax.axis_size("xy"))
    r, jd, jo, bi = dense(right_side), dense(jac_diag), dense(jac_off), dense(block_inv)
    pw, pd, po = dense(press_weight), dense(press_diag), dense(press_off)
    wi, ag = dense(well_index), dense(agg_map)
    op = level1_op.astype(F32)
    lv = jnp.concatenate([jnp.stack([op[a, a] for a in range(AGG)]), jnp.sum(op, axis=0)])
    lv = lv.transpose(1, 3, 2, 0).reshape(2, ROWS, 2 * AGG)
    jd0, jo0 = jd[:, 0], jo[:, :, 0]
    vec, field, plane = (NC, 2, ROWS, LANES), (2, ROWS, LANES), (ROWS, LANES)
    gz, xy = sizes

    def bind(body, *static):
        def kernel(*refs):
            return body(*static, *refs)

        return kernel

    given = (r, jd, jo, bi, pw, pd, po, wi, ag, lv, jd0, jo0)

    def run(body, outs, *args, **kw):
        args = [a if any(a is b for b in given) else near_by(a) for a in args]
        return call(body, outs, [VMEM] * len(args), args, **kw)

    def many(size, parts):
        return (size, parts, ROWS, LANES)

    rhs, fg, *msgs, wc, inv = call(
        first_kernel, [field, field] + [(6, ROWS, LANES)] * 4 + [field, (4, ROWS, LANES)],
        [SMEM] + [VMEM] * 6, (well_columns, r, pw, pd, wi, ag, coarsest_inv.reshape(64, 64)),
    )
    fixed = rings(msgs)
    part, rows, buf = run(
        bind(first_coarse_kernel, sizes), [field, (2 * gz, LANES), many(gz, 4)],
        fg, rhs, wi, *fixed, pd, po, ag, lv,
    )
    shapes = [(7, NC, 2, ROWS, LANES)]
    for step in range(2):
        later = step == 1
        if later:
            got_z = spread(rows.reshape(gz, 2, LANES), "gz", (2 * gz, LANES))
            (buf,) = run(second_relay_kernel, [(2 * xy, LANES)], got_z, rows)
        else:
            buf, wsums, got_z = run(
                first_relay_kernel, [(2 * xy, LANES), (3, ROWS, LANES), (2 * gz, LANES)],
                spread(buf, "gz"), rows,
            )
        got = spread(buf.reshape(xy, 2, LANES), "xy", (2 * xy, LANES))
        p, buf, *msgs, tops = run(
            bind(pressure_kernel, sizes, later), [field, many(gz, 2), plane, plane, plane],
            got, got_z, inv, *fixed, halo if later else inv, part, rhs, pd, po, wi,
        )
        xlo, xhi = rings([None, None, *msgs])
        got = spread(buf, "gz")
        side = (NC, ROWS, LANES)
        wide = side if later else (NC + 1, ROWS, LANES)
        more = (tops, d0, level0) if later else ()
        d, *msgs, column = run(
            bind(direction_kernel, sizes, later), [vec, side, side, wide, wide, plane],
            w0 if later else r, p, got, xlo, xhi, jd0, jo0, bi, wc, wsums, wi, *more,
        )
        sides = rings(msgs)
        scratch = [pltpu.VMEM(s, F32) for s in shapes]
        if later:
            d1 = d
            w1, buf = run(
                bind(image_kernel, sizes, later), [vec, many(gz, 6)],
                d, *sides, column, jd, jo, wc, r, w0, tops, level0, scratch_shapes=scratch,
            )
        else:
            d0 = d
            w0, buf, rhs, fg, *msgs, dots = run(
                bind(image_kernel, sizes, later),
                [vec, many(gz, 4), field, field, plane, plane, plane],
                d, *sides, column, jd, jo, wc, r, pw, pd, scratch_shapes=scratch,
            )
            xlo, xhi = rings([None, None, *msgs])
            got = spread(buf, "gz")
            part, rhs, halo, level0, rows = run(
                bind(second_coarse_kernel, sizes),
                [field, field, (4, ROWS, LANES), plane, (2 * gz, LANES)],
                fg, rhs, r, w0, wc, pw, wsums, got, xlo, xhi, *fixed, dots, pd, po, ag, lv,
            )
    got = spread(buf, "gz")
    buf, level1 = run(close_kernel, [(xy, LANES), plane], got, wsums)
    got = spread(buf.reshape(xy, 1, LANES), "xy", (xy, LANES))
    solution, residual, hessenberg = run(
        last_kernel, [vec, vec, (2, 3)], got, tops, r, d0, w0, d1, w1, wc, level0, level1, fast=False
    )
    return undense(solution), undense(residual), hessenberg.T


def solution(mesh):
    return jax.shard_map(
        on_device,
        mesh=mesh,
        in_specs=(
            P(None, "gz", "xy", None),
            P(None, None, "gz", "xy", None),
            P(None, None, None, "gz", "xy", None),
            P(None, None, "gz", "xy", None),
            P(None, "gz", "xy", None),
            P("gz", "xy", None),
            P(None, "gz", "xy", None),
            P("gz", "xy", None),
            P(),
            P("gz", "xy", None),
            P(None, None, "gz", "xy", None),
            P("gz", "xy", None, None),
        ),
        out_specs=(P(None, "gz", "xy", None), P(None, "gz", "xy", None), P()),
        check_vma=False,
    )
```

```python
import jax
import jax.numpy as jnp
from jax import lax
from jax.experimental import pallas as pl
from jax.experimental.pallas import tpu as pltpu
from jax.sharding import PartitionSpec as P

EPSILON = 1e-06
NC = 12
AGG = 8
F32 = jnp.float32
ROWS, LANES = 8, 128
VMEM = pl.BlockSpec(memory_space=pltpu.VMEM)
SMEM = pl.BlockSpec(memory_space=pltpu.SMEM)
HBM = pl.BlockSpec(memory_space=pltpu.HBM)


def dense(a):
    s = a.shape[:-2]
    n = len(s)
    a = jnp.swapaxes(a.reshape(s + (2, 4, LANES)), n, n + 1)
    return a.reshape(s + (ROWS, LANES))


def undense(a):
    s = a.shape[:-2]
    n = len(s)
    a = jnp.swapaxes(a.reshape(s + (4, 2, LANES)), n, n + 1)
    return a.reshape(s + (2, 4 * LANES))


def grids():
    return (
        lax.broadcasted_iota(jnp.int32, (ROWS, LANES), 0),
        lax.broadcasted_iota(jnp.int32, (ROWS, LANES), 1),
    )


def even_rows():
    return (grids()[0] & 1) == 0


def turn(a, shift, axis):
    return pltpu.roll(a, shift % a.shape[axis], axis)


def pack_low(f):
    return jnp.where(even_rows(), f[0], turn(f[1], 1, 0))


def pack_high(f):
    return jnp.where(even_rows(), turn(f[0], -1, 0), f[1])


def along_y(f):
    row, lane = grids()
    t = turn(f, 1, 1)
    before = jnp.where(lane == 0, jnp.where(row < 2, 0.0, turn(t, 2, 0)), t)
    t = turn(f, -1, 1)
    after = jnp.where(lane == LANES - 1, jnp.where(row >= ROWS - 2, 0.0, turn(t, -2, 0)), t)
    return before, after


def near(f, zlo, zhi, xlo, xhi):
    even = even_rows()
    y0, y1 = along_y(f[0]), along_y(f[1])
    xm = (
        jnp.where(even, xlo, turn(f[0], 1, 0)),
        jnp.where(even, turn(xlo, -1, 0), turn(f[1], 1, 0)),
    )
    xp = (
        jnp.where(even, turn(f[0], -1, 0), turn(xhi, 1, 0)),
        jnp.where(even, turn(f[1], -1, 0), xhi),
    )
    return ((zlo, f[0]), (f[1], zhi), xm, xp, (y0[0], y1[0]), (y0[1], y1[1]))


def position():
    return lax.axis_index("gz"), lax.axis_index("xy")


def edges(sizes, halos):
    g, s = position()
    ok = (g > 0, g < sizes[0] - 1, s > 0, s < sizes[1] - 1)
    return [jnp.where(o, h, 0.0) for o, h in zip(ok, halos)]


def total(a):
    return jnp.sum(jnp.sum(a, axis=0, keepdims=True), axis=1, keepdims=True)


def scalar_stencil(f, halos, pd, po):
    nb = near(f, *halos)
    out = []
    for z in range(2):
        t = pd[z].astype(F32) * f[z]
        for k in range(6):
            t = t + po[k, z].astype(F32) * nb[k][z]
        out.append(t)
    return out


def summed(got, q):
    t = got[0, q]
    for m in range(1, got.shape[0]):
        t = t + got[m, q]
    return t


def beside_z(sizes, got, q, below):
    g, _ = position()
    return got[jnp.maximum(g - 1, 0) if below else jnp.minimum(g + 1, sizes[0] - 1), q]


def packed(levels):
    return pack_high([levels[0]] * 2), pack_low([levels[1]] * 2)


def call(body, outs, ins, args, fast=True, **kw):
    return pl.pallas_call(
        body,
        out_shape=[pltpu.VMEM(o, F32) if fast else jax.ShapeDtypeStruct(o, F32) for o in outs],
        in_specs=ins,
        out_specs=[VMEM] * len(outs),
        **kw,
    )(*args)


def near_by(a):
    return pltpu.with_memory_space_constraint(a, pltpu.VMEM)


def rings(msgs):
    out = []
    for m, (axis, step) in zip(msgs, (("gz", 1), ("gz", -1), ("xy", 0), ("xy", 1))):
        if m is None:
            continue
        n = lax.axis_size(axis)
        if axis == "gz":
            pairs = [(i, (i + step) % n) for i in range(n)]
        else:
            pairs = [(i, (((i + step) ^ 1) - step) % n) for i in range(n)]
        out.append(near_by(lax.ppermute(m, axis, pairs)))
    return out


def is_even():
    return (position()[1] & 1) == 0


def to_sides(first, second, at, up, down):
    even = is_even()
    first[at] = jnp.where(even, up, down)
    second[at] = jnp.where(even, down, up)


def from_sides(first, second):
    even = is_even()

    def low(at=...):
        return jnp.where(even, second[at], first[at])

    def high(at=...):
        return jnp.where(even, first[at], second[at])

    return low, high


def spread(buf, axis, shape=None):
    got = lax.all_to_all(buf, axis, 0, 0, tiled=True)
    return near_by(got if shape is None else got.reshape(shape))


def guess_of(v, pw, pd, rhs_ref, fg_ref):
    fg = []
    for z in range(2):
        t = pw[0, z].astype(F32) * v[0][z]
        for i in range(1, NC):
            t = t + pw[i, z].astype(F32) * v[i][z]
        rhs_ref[z] = t
        fg.append(t / pd[z].astype(F32))
        fg_ref[z] = fg[z]
    return fg


def order_inverse(inv, inv_ref):
    col = lax.broadcasted_iota(jnp.int32, (64, LANES), 0)
    lane = lax.broadcasted_iota(jnp.int32, (64, LANES), 1)
    wanted = 2 * (lane >> 5) + (lane & 1)
    mine = (col & 15) == ((lane & 31) >> 1)
    for m in range(ROWS):
        pick = jnp.where(col == 8 * m + wanted, 1.0, 0.0).astype(jnp.bfloat16)
        t = jnp.dot(inv[...], pick, preferred_element_type=F32)
        t = jnp.where(mine, t, 0.0)
        for n in range(4):
            inv_ref[n, m : m + 1, :] = jnp.sum(t[16 * n : 16 * n + 16], axis=0, keepdims=True)


def in_one_row(values):
    return jnp.sum(pltpu.roll(values, 0, 1, stride=16, stride_axis=0), axis=0, keepdims=True)


def in_rows(row):
    at, _ = grids()
    t = jnp.broadcast_to(row, (ROWS, LANES))
    for bit in (1, 2, 4):
        t = jnp.where((at & bit) != 0, turn(t, -16 * bit, 1), t)
    return t


def two_rows(ref, first, second):
    at = lax.broadcasted_iota(jnp.int32, ref.shape, 0)
    ref[...] = jnp.where((at & 1) == 0, first, second)


GUESS, INVERSE, AGGREGATE, SHARE, WEIGHT = 0, 1, 3, 4, 5


def stash_kernel(jo, jd, *refs):
    *refs, sems = refs
    n = len(refs) // 2 - 1
    sources = [jo.at[:, :, 0], jd.at[:, 0], *refs[:n]]
    copies = [pltpu.make_async_copy(a, b, sems.at[m]) for m, (a, b) in enumerate(zip(sources, refs[n:]))]
    for c in copies:
        c.start()
    for c in copies:
        c.wait()


def stash(jo, jd, *arrays):
    kept = [
        jax.ShapeDtypeStruct(jo.shape[:2] + jo.shape[3:], jo.dtype),
        jax.ShapeDtypeStruct(jd.shape[:1] + jd.shape[2:], jd.dtype),
        *arrays,
    ]
    return pl.pallas_call(
        stash_kernel,
        out_shape=[pltpu.VMEM(a.shape, a.dtype) for a in kept],
        in_specs=[HBM] * len(kept),
        out_specs=[VMEM] * len(kept),
        scratch_shapes=[pltpu.SemaphoreType.DMA((len(kept),))],
    )(jo, jd, *arrays)


def first_kernel(
    cols, r, pw, pd, po, wi, ag, inv, rhs_ref, fg_ref, up_z, down_z, up_x, down_x, wc_ref, inv_ref,
    pd_ref, po_ref, wi_ref, ag_ref,
):
    v = [[r[i, z] for z in range(2)] for i in range(NC)]
    fg = guess_of(v, pw, pd, rhs_ref, fg_ref)
    order_inverse(inv, inv_ref)
    row, lane = grids()
    _, s = position()
    here = (2 * s + (row & 1)) * 512 + (row >> 1) * LANES + lane
    count = jnp.zeros((ROWS, LANES), F32)
    for w in range(cols.shape[0]):
        count = count + jnp.where(here == cols[w], 1.0, 0.0)
    wc = [wi[z] * count for z in range(2)]
    for z in range(2):
        wc_ref[z] = wc[z]
    share = [pw[0, z].astype(F32) * wc[z] / pd[z].astype(F32) for z in range(2)]
    agg = [ag[z].astype(F32) for z in range(2)]
    for z in range(2):
        pd_ref[z] = pd[z].astype(F32)
        wi_ref[z] = wi[z]
        ag_ref[z] = agg[z]
        for k in range(6):
            po_ref[k, z] = po[k, z].astype(F32)
    weight = wi[0] + wi[1]
    def planes(pick, pair):
        return [pick(fg), inv_ref[pair[0]], inv_ref[pair[1]], pick(agg), pick(share), weight]

    for m, t in enumerate(planes(lambda f: f[1], (2, 3))):
        up_z[m] = t
    for m, t in enumerate(planes(lambda f: f[0], (0, 1))):
        down_z[m] = t
    for m, (up, down) in enumerate(zip(planes(pack_high, (1, 3)), planes(pack_low, (0, 2)))):
        to_sides(up_x, down_x, m, up, down)


def coarse_body(fg, rhs, halos, pd, po, ag, lv, part_ref):
    applied = scalar_stencil(fg, halos, pd, po)
    _, lane = grids()
    even = (lax.broadcasted_iota(jnp.int32, (ROWS, 1), 0) & 1) == 0
    g, s = position()
    place = 32 * (s & 3) + 4 * g
    tile = jnp.zeros((1, LANES), F32)
    at = lax.broadcasted_iota(jnp.int32, (1, LANES), 1)
    values = jnp.zeros((ROWS, LANES), F32)
    for z in range(2):
        rest = rhs[z] - applied[z]
        level = lv[z]
        guess = fg[z]
        sums = jnp.zeros((ROWS, 1), F32)
        for a in range(AGG):
            mine = ag[z] == a
            c = jnp.sum(jnp.where(mine, rest, 0.0), axis=1, keepdims=True)
            value = c / level[:, a : a + 1]
            guess = guess + jnp.where(mine, value, 0.0)
            sums = sums + (c - level[:, AGG + a : AGG + a + 1] * value)
            values = values + jnp.where(lane == AGG * z + a, value, 0.0)
        part_ref[z] = guess
        for x in range(2):
            t = jnp.sum(jnp.where(even if x == 0 else ~even, sums, 0.0), axis=0, keepdims=True)
            tile = tile + jnp.where(at == place + 2 * z + x, t, 0.0)
    return tile, in_one_row(values)


def first_coarse_kernel(sizes, fg, rhs, wi, zlo, zhi, xlo, xhi, pd, po, ag, lv, part_ref, rows_ref, buf):
    xlo, xhi = from_sides(xlo, xhi)
    halos = edges(sizes, [zlo[GUESS], zhi[GUESS], xlo(GUESS), xhi(GUESS)])
    tile, values = coarse_body([fg[0], fg[1]], rhs, halos, pd, po, ag, lv, part_ref)
    two_rows(rows_ref, tile, values)
    weight = wi[0] + wi[1]
    for m in range(buf.shape[0]):
        buf[m, 0] = rows_ref[0:ROWS]
        buf[m, 1] = weight
        buf[m, 2] = xlo(WEIGHT)
        buf[m, 3] = xhi(WEIGHT)


def second_coarse_kernel(
    sizes, fg, rhs, r, w, wc, pw, wsums, got, xlo, xhi, szlo, szhi, sxlo, sxhi, dots, pd, po, ag, lv,
    part_ref, rhs_ref, halo_ref, level_ref, rows_ref,
):
    xlo, xhi = from_sides(xlo, xhi)
    sxlo, sxhi = from_sides(sxlo, sxhi)
    level = summed(got, 1) / wsums[0]
    level_ref[...] = level
    sides = packed([summed(got, 2) / wsums[1], summed(got, 3) / wsums[2]])
    halos = [
        beside_z(sizes, got, 0, True) - szlo[SHARE] * level,
        beside_z(sizes, got, 0, False) - szhi[SHARE] * level,
        xlo() - sxlo(SHARE) * sides[0],
        xhi() - sxhi(SHARE) * sides[1],
    ]
    halos = edges(sizes, halos)
    for n in range(4):
        halo_ref[n] = halos[n]
    rhs_now, fg_now = [], []
    first = second = jnp.zeros((ROWS, LANES), F32)
    for z in range(2):
        fall = wc[z] * level
        t = rhs[z] - pw[0, z].astype(F32) * fall
        rhs_ref[z] = t
        rhs_now.append(t)
        fg_now.append(t / pd[z].astype(F32))
        first = first + r[0, z] * fall
        second = second + (2.0 * w[0, z] - fall) * fall
    tile, values = coarse_body(fg_now, rhs_now, halos, pd, po, ag, lv, part_ref)
    _, s = position()
    lane = lax.broadcasted_iota(jnp.int32, (1, LANES), 1)
    sums = dots[0:1]
    for m, t in ((1, first), (2, second)):
        sums = sums - jnp.where(lane == m, total(t), 0.0)
    two_rows(rows_ref, tile + pltpu.roll(sums, 32 * ((s + 1) & 3), 1), values)


def relay(rows, own, out_ref):
    at = lax.broadcasted_iota(jnp.int32, rows.shape, 0)
    tile = jnp.sum(jnp.where((at & 1) == 0, rows, 0.0), axis=0, keepdims=True)
    two_rows(out_ref, tile, own)


def first_relay_kernel(got, own, out_ref, sums_ref, rows_ref):
    for m in range(got.shape[0]):
        rows_ref[2 * m : 2 * m + 2] = got[m, 0, 0:2]
    relay(rows_ref[...], own[1:2], out_ref)
    for n in range(3):
        sums_ref[n] = summed(got, 1 + n)


def second_relay_kernel(got, own, out_ref):
    relay(got[...], own[1:2], out_ref)


def pressure_kernel(sizes, later, got, got_z, inv, zlo, zhi, xlo, xhi, halo, part, rhs, pd, po, wi,
                    p_ref, buf, up_x, down_x, tops_ref):
    even = even_rows()
    _, s = position()
    g, _ = position()
    _, lane = grids()
    t = tops = jnp.zeros((ROWS, LANES), F32)
    for k in range(4):
        some = got[pl.ds(2 * k, ROWS, stride=8), :]
        t = t + jnp.where((lane >> 5) == k, some, 0.0)
        tops = tops + turn(some, -32 * ((k + 1) % 4), 1)
    tops_ref[...] = tops
    own = []
    for z in range(2):
        pair = [total(inv[2 * z + x] * t) for x in range(2)]
        own.append(jnp.where(even, pair[0], pair[1]))
    low = in_rows(got[pl.ds(2 * jnp.maximum(s - 1, 0) + 1, 1), :])
    high = in_rows(got[pl.ds(2 * jnp.minimum(s + 1, sizes[1] - 1) + 1, 1), :])
    below = in_rows(got_z[pl.ds(2 * jnp.maximum(g - 1, 0) + 1, 1), :])
    above = in_rows(got_z[pl.ds(2 * jnp.minimum(g + 1, sizes[0] - 1) + 1, 1), :])
    low_even, high_odd = turn(low, -1, 0), turn(high, 1, 0)
    halos = []
    sides = (lambda at: zlo[at], lambda at: zhi[at], *from_sides(xlo, xhi))
    for n, side in enumerate(sides):
        c = [total(side(INVERSE + m) * t) for m in range(2)]
        h = halo[n] if later else side(GUESS)
        h = h + jnp.where(even, c[0], c[1])
        agg = side(AGGREGATE)
        for a in range(AGG):
            one, two = slice(a, a + 1), slice(AGG + a, AGG + a + 1)
            value = (
                below[:, two],
                above[:, one],
                jnp.where(even, low_even[:, one], low[:, two]),
                jnp.where(even, high[:, one], high_odd[:, two]),
            )[n]
            h = h + jnp.where(agg == float(a), value, 0.0)
        halos.append(h)
    halos = edges(sizes, halos)
    f = [part[z] + own[z] for z in range(2)]
    applied = scalar_stencil(f, halos, pd, po)
    p = []
    for z in range(2):
        p.append(f[z] + (rhs[z] - applied[z]) / pd[z].astype(F32))
        p_ref[z] = p[z]
    to_sides(up_x, down_x, ..., pack_high(p), pack_low(p))
    column = wi[0] * p[0] + wi[1] * p[1]
    for m in range(buf.shape[0]):
        buf[m, 0] = jnp.where(g < m, p[1], p[0])
        buf[m, 1] = column


def steps_of(tops):
    rr, rw, ww = (total(tops[:, m : m + 1]) for m in range(3))
    beta = jnp.sqrt(rr + EPSILON)
    h00 = rw / (beta * beta)
    rest = jnp.maximum(ww / (beta * beta) - h00 * h00, 0.0)
    return beta, h00, jnp.sqrt(rest + EPSILON)


def direction_kernel(sizes, later, v, p, got, hxlo, hxhi, jd, jo, bi, wc, wsums, wi, *more):
    if later:
        tops, d0, old, *more = more
        beta, h00, h10 = steps_of(tops)
        scale = 1.0 / (beta * h10)
    d_ref, up_z, down_z, up_x, down_x, column_ref = more
    f = [p[0], p[1]]
    halos = [beside_z(sizes, got, 0, True), beside_z(sizes, got, 0, False), *[h() for h in from_sides(hxlo, hxhi)]]
    nb = near(f, *edges(sizes, halos))
    level = summed(got, 1) / wsums[0]
    rem = []
    for i in range(NC):
        pair = []
        for z in range(2):
            t = jd[i, z].astype(F32) * f[z]
            for k in range(6):
                t = t + jo[k, i, z].astype(F32) * nb[k][z]
            if i == 0:
                t = t + wc[z] * (f[z] - level)
                if later:
                    t = t + wc[z] * old[...]
            pair.append(v[i, z] - t)
        rem.append(pair)
    for i in range(NC):
        pair = []
        for z in range(2):
            ts = [None, None]
            for j in range(NC):
                u = bi[i, j, z].astype(F32) * rem[j][z]
                ts[j % 2] = u if ts[j % 2] is None else ts[j % 2] + u
            t = ts[0] + ts[1]
            if i == 0:
                t = t + f[z]
            if later:
                t = (t - h00 * d0[i, z]) * scale
            d_ref[i, z] = t
            pair.append(t)
        up_z[i] = pair[1]
        down_z[i] = pair[0]
        to_sides(up_x, down_x, i, pack_high(pair), pack_low(pair))
        if i == 0:
            column = wi[0] * pair[0] + wi[1] * pair[1]
            column_ref[...] = column
            if not later:
                up_x[NC] = column
                down_x[NC] = column


def image_kernel(sizes, later, jo_far, jd_far, d, zlo, zhi, xlo, xhi, column, wc, r, *more):
    *more, nb, jo, jd, sems = more
    xlo, xhi = from_sides(xlo, xhi)
    if later:
        w0, tops, old, w_ref, buf = more
    else:
        pw, pd, w_ref, buf, rhs_ref, fg_ref, up_x, down_x, dots_ref = more

    def rows_of(i):
        return (
            pltpu.make_async_copy(jo_far.at[:, i], jo.at[:, i], sems.at[0, i]),
            pltpu.make_async_copy(jd_far.at[i], jd.at[i], sems.at[1, i]),
        )

    for i in range(NC):
        for copy in rows_of(i):
            copy.start()
    for j in range(NC):
        f = [d[j, 0], d[j, 1]]
        n = near(f, *edges(sizes, [zlo[j], zhi[j], xlo(j), xhi(j)]))
        for z in range(2):
            nb[0, j, z] = f[z]
            for k in range(6):
                nb[k + 1, j, z] = n[k][z]

    def row(i, carry):
        for copy in rows_of(i):
            copy.wait()
        for z in range(2):
            ts = [None] * 4
            for k in range(7):
                for j in range(NC):
                    c = (jd[i, j, z] if k == 0 else jo[k - 1, i, j, z]).astype(F32)
                    u = c * nb[k, j, z]
                    q = j % 4
                    ts[q] = u if ts[q] is None else ts[q] + u
            w_ref[i, z] = (ts[0] + ts[1]) + (ts[2] + ts[3])
        return carry

    lax.fori_loop(0, NC, row, 0)
    for z in range(2):
        w_ref[0, z] = w_ref[0, z] + wc[z] * d[0, z]
    row_at, lane = grids()
    zero = jnp.zeros((ROWS, LANES), F32)
    sums = [zero, zero, zero]
    falls = [zero] * 4
    if later:
        beta, h00, h10 = steps_of(tops)
        scale = 1.0 / (beta * h10)
    for i in range(NC):
        for z in range(2):
            w = w_ref[i, z]
            if later:
                before = w0[i, z] - wc[z] * old[...] if i == 0 else w0[i, z]
                b0 = r[i, z] * (1.0 / beta)
                b1 = (before - h00 * r[i, z]) * scale
                first, second = w * b0, w * b1
                if i == 0:
                    falls = [t + wc[z] * u for t, u in zip(falls, (b0, b1, w, wc[z]))]
            else:
                first, second = r[i, z] * r[i, z], w * r[i, z]
            sums = [sums[0] + first, sums[1] + second, sums[2] + w * w]
    t = zero
    for m in range(3):
        t = t + jnp.where((row_at == 0) & (lane == m), total(sums[m]), 0.0)
    if later:
        for m in range(buf.shape[0]):
            buf[m, 0] = t
            buf[m, 1] = column[...]
            for n in range(4):
                buf[m, 2 + n] = falls[n]
    else:
        dots_ref[...] = t
        v = [[w_ref[i, z] for z in range(2)] for i in range(NC)]
        fg = guess_of(v, pw, pd, rhs_ref, fg_ref)
        to_sides(up_x, down_x, ..., pack_high(fg), pack_low(fg))
        below, above = edges(sizes, [zero, zero, xlo(NC), xhi(NC)])[2:]
        g, _ = position()
        for m in range(buf.shape[0]):
            buf[m, 0] = jnp.where(g < m, fg[1], fg[0])
            buf[m, 1] = column[...]
            buf[m, 2] = below
            buf[m, 3] = above


def close_kernel(got, wsums, buf, level_ref):
    row, lane = grids()
    level = summed(got, 1) / wsums[0]
    level_ref[...] = level
    falls = [summed(got, 2 + n) for n in range(4)]
    t = summed(got, 0)
    for m, fall in enumerate((falls[0], falls[1], 2.0 * falls[2] - falls[3] * level)):
        t = t - jnp.where((row == 0) & (lane == m), total(fall * level), 0.0)
    buf[...] = jnp.broadcast_to(t[0:1], buf.shape)


def last_kernel(got, tops, r, d0, w0, d1, w1, wc, level0, level1, sol_ref, res_ref, hess_ref):
    t = jnp.sum(got[...], axis=0, keepdims=True)
    h01, h11, norm = (t[:, m : m + 1] for m in range(3))
    beta, h00, h10 = steps_of(tops)
    h21 = jnp.sqrt(jnp.maximum(norm - h01 * h01 - h11 * h11, 0.0) + EPSILON)
    radius = jnp.sqrt(h00 * h00 + h10 * h10)
    c0, s0 = h00 / radius, h10 / radius
    u00, u01, u11 = radius, c0 * h01 + s0 * h11, c0 * h11 - s0 * h01
    t0, t1 = c0 * beta, -s0 * beta
    radius = jnp.sqrt(u11 * u11 + h21 * h21)
    t1 = (u11 / radius) * t1
    y1 = t1 / radius
    y0 = (t0 - u01 * y1) / u00
    y0 = y0 / beta
    for i in range(NC):
        for z in range(2):
            sol_ref[i, z] = y0 * d0[i, z] + y1 * d1[i, z]
            t = y0 * w0[i, z] + y1 * w1[i, z]
            if i == 0:
                t = t - wc[z] * (y0 * level0[...] + y1 * level1[...])
            res_ref[i, z] = r[i, z] - t
    col = lax.broadcasted_iota(jnp.int32, (2, 3), 0)
    at = lax.broadcasted_iota(jnp.int32, (2, 3), 1)
    h = jnp.zeros((2, 3), F32)
    for i, j, value in ((0, 0, h00), (1, 0, h10), (0, 1, h01), (1, 1, h11), (2, 1, h21)):
        h = h + jnp.where((at == i) & (col == j), value, 0.0)
    hess_ref[...] = h


def on_device(
    right_side, jac_diag, jac_off, block_inv, press_weight, press_diag, press_off, well_index,
    well_columns, agg_map, level1_op, coarsest_inv,
):
    sizes = (lax.axis_size("gz"), lax.axis_size("xy"))
    r, jd, jo, bi = dense(right_side), dense(jac_diag), dense(jac_off), dense(block_inv)
    pw, pd, po = dense(press_weight), dense(press_diag), dense(press_off)
    wi, ag = dense(well_index), dense(agg_map)
    op = level1_op.astype(F32)
    lv = jnp.concatenate([jnp.stack([op[a, a] for a in range(AGG)]), jnp.sum(op, axis=0)])
    lv = lv.transpose(1, 3, 2, 0).reshape(2, ROWS, 2 * AGG)
    vec, field, plane = (NC, 2, ROWS, LANES), (2, ROWS, LANES), (ROWS, LANES)
    gz, xy = sizes

    def bind(body, *static):
        def kernel(*refs):
            return body(*static, *refs)

        return kernel

    far = (jo, jd)


    def run(body, outs, *args, **kw):
        away = [any(a is b for b in far) for a in args]
        specs = [HBM if b else VMEM for b in away]
        args = [a if b or a is lv else near_by(a) for a, b in zip(args, away)]
        return call(body, outs, specs, args, **kw)

    def many(size, parts):
        return (size, parts, ROWS, LANES)

    rhs, fg, *msgs, wc, inv, pd, po, wi, ag = call(
        first_kernel,
        [field, field] + [(6, ROWS, LANES)] * 4
        + [field, (4, ROWS, LANES), field, (6, 2, ROWS, LANES), field, field],
        [SMEM] + [VMEM] * 7, (well_columns, r, pw, pd, po, wi, ag, coarsest_inv.reshape(64, 64)),
    )
    fixed = rings(msgs)
    jo0, jd0, bi, r, pw = stash(jo, jd, bi, r, pw)
    part, rows, buf = run(
        bind(first_coarse_kernel, sizes), [field, (2 * gz, LANES), many(gz, 4)],
        fg, rhs, wi, *fixed, pd, po, ag, lv,
    )
    for step in range(2):
        later = step == 1
        if later:
            got_z = spread(rows.reshape(gz, 2, LANES), "gz", (2 * gz, LANES))
            (buf,) = run(second_relay_kernel, [(2 * xy, LANES)], got_z, rows)
        else:
            buf, wsums, got_z = run(
                first_relay_kernel, [(2 * xy, LANES), (3, ROWS, LANES), (2 * gz, LANES)],
                spread(buf, "gz"), rows,
            )
        got = spread(buf.reshape(xy, 2, LANES), "xy", (2 * xy, LANES))
        p, buf, *msgs, tops = run(
            bind(pressure_kernel, sizes, later), [field, many(gz, 2), plane, plane, plane],
            got, got_z, inv, *fixed, halo if later else inv, part, rhs, pd, po, wi,
        )
        xlo, xhi = rings([None, None, *msgs])
        got = spread(buf, "gz")
        side = (NC, ROWS, LANES)
        wide = side if later else (NC + 1, ROWS, LANES)
        more = (tops, d0, level0) if later else ()
        d, *msgs, column = run(
            bind(direction_kernel, sizes, later), [vec, side, side, wide, wide, plane],
            w0 if later else r, p, got, xlo, xhi, jd0, jo0, bi, wc, wsums, wi, *more,
        )
        sides = rings(msgs)
        scratch = [
            pltpu.VMEM((7, NC, 2, ROWS, LANES), F32),
            pltpu.VMEM(jo.shape, jo.dtype),
            pltpu.VMEM(jd.shape, jd.dtype),
            pltpu.SemaphoreType.DMA((2, NC)),
        ]
        if later:
            d1 = d
            w1, buf = run(
                bind(image_kernel, sizes, later), [vec, many(gz, 6)],
                jo, jd, d, *sides, column, wc, r, w0, tops, level0, scratch_shapes=scratch,
            )
        else:
            d0 = d
            w0, buf, rhs, fg, *msgs, dots = run(
                bind(image_kernel, sizes, later),
                [vec, many(gz, 4), field, field, plane, plane, plane],
                jo, jd, d, *sides, column, wc, r, pw, pd, scratch_shapes=scratch,
            )
            xlo, xhi = rings([None, None, *msgs])
            got = spread(buf, "gz")
            part, rhs, halo, level0, rows = run(
                bind(second_coarse_kernel, sizes),
                [field, field, (4, ROWS, LANES), plane, (2 * gz, LANES)],
                fg, rhs, r, w0, wc, pw, wsums, got, xlo, xhi, *fixed, dots, pd, po, ag, lv,
            )
    got = spread(buf, "gz")
    buf, level1 = run(close_kernel, [(xy, LANES), plane], got, wsums)
    got = spread(buf.reshape(xy, 1, LANES), "xy", (xy, LANES))
    solution, residual, hessenberg = run(
        last_kernel, [vec, vec, (2, 3)], got, tops, r, d0, w0, d1, w1, wc, level0, level1, fast=False
    )
    return undense(solution), undense(residual), hessenberg.T


def solution(mesh):
    return jax.shard_map(
        on_device,
        mesh=mesh,
        in_specs=(
            P(None, "gz", "xy", None),
            P(None, None, "gz", "xy", None),
            P(None, None, None, "gz", "xy", None),
            P(None, None, "gz", "xy", None),
            P(None, "gz", "xy", None),
            P("gz", "xy", None),
            P(None, "gz", "xy", None),
            P("gz", "xy", None),
            P(),
            P("gz", "xy", None),
            P(None, None, "gz", "xy", None),
            P("gz", "xy", None, None),
        ),
        out_specs=(P(None, "gz", "xy", None), P(None, "gz", "xy", None), P()),
        check_vma=False,
    )
```
